32 devices in a mesh: section: 4 (over z), row: 8 (over y, x, core).
Axes of the slice: x: 2, y: 2, z: 4, core: 2. Of those that a mesh axis runs over, the one named last changes fastest.
Arguments:
- features: bfloat16 [16, 16, 16, 192], P(None, 'row'), may hold values from -6 to 6
- norm_gain: float32 [4, 192], P('section'), may hold values from 0.5 to 1.5
- conv_weight: bfloat16 [4, 3, 3, 3, 192, 192], P('section'), may hold values from -0.078125 to 0.078125
- conv_bias: float32 [4, 192], P('section'), may hold values from -2.5 to 2.5
Outputs:
- decoded: bfloat16 [16, 16, 16, 192], P('section', 'row')
The draws below stay inside these ranges and needn't reach their ends.
All inputs are finite; a program needn't handle non-finite values.
Results may differ from the reference program's by a relative error of at most 0.03.
Values may be sent and summed in bfloat16 or wider, within the bound.
A program may use at most 64 MiB of HBM per device.

```python
import jax
import jax.numpy as jnp
from jax import lax

C = 192
COLS = 16
LAYERS = 4
FRAMES_ALL = 16
ROWS = 16


def block_levels(stream_key, dims, shards, low, top_value):
    gain, own = 1.0, jax.random.fold_in(stream_key, 6)
    for dim, shards_of in shards:
        steps = jnp.exp(jax.random.uniform(jax.random.fold_in(own, dim), (shards_of,), jnp.float32, low / len(shards), top_value / len(shards)))
        gain = gain * jnp.repeat(steps, dims[dim] // shards_of).reshape([-1 if axis == dim else 1 for axis in range(len(dims))])
    return gain


def centred(rng, extent, width, most, pieces=(), kind=jnp.bfloat16):
    result = width * jax.random.normal(rng, extent, jnp.float32)
    if pieces:
        result = result * block_levels(rng, extent, pieces, -0.22, 0.18)
    return jnp.clip(result, -most, most).astype(kind)


def setup_inputs(seed: int = 0) -> dict:
    splits = jax.random.split(jax.random.key(seed), 5)
    return {
        "features": centred(splits[0], (FRAMES_ALL, ROWS, COLS, C), 1.0, 6.0, ((1, 8),)),
        "norm_gain": jnp.clip(1.0 + 0.1 * jax.random.normal(splits[1], (LAYERS, C), jnp.float32), 0.5, 1.5),
        "conv_weight": centred(splits[2], (LAYERS, 3, 3, 3, C, C), (27 * C) ** -0.5, 0.078125, ((0, 4),)),
        "conv_bias": centred(splits[3], (LAYERS, C), 0.3, 2.5, ((0, 4),), jnp.float32),
    }


def reference(features, norm_gain, conv_weight, conv_bias):
    state = features
    for layer in range(LAYERS):
        wide = state.astype(jnp.float32)
        square = lax.optimization_barrier(jnp.mean(wide * wide, axis=-1, keepdims=True))
        normed = jax.nn.silu(wide * lax.rsqrt(square + 1e-06) * norm_gain[layer]).astype(jnp.bfloat16)
        padded = jnp.pad(normed, ((2, 0), (1, 1), (1, 1), (0, 0))).astype(jnp.float32)
        kernel = conv_weight[layer].astype(jnp.float32)
        conv = lax.conv_general_dilated(padded[None], kernel, (1, 1, 1), 'VALID', dimension_numbers=('NDHWC', 'DHWIO', 'NDHWC'), preferred_element_type=jnp.float32)[0]
        state = (wide + conv + conv_bias[layer]).astype(jnp.bfloat16)
    return state
```

```python
import functools

import jax
import jax.numpy as jnp
from jax import lax
from jax.experimental import pallas as pl
from jax.experimental.pallas import tpu as pltpu
from jax.sharding import PartitionSpec as P

FRAMES = 2
LANES = 128
MESH = pl.DeviceIdType.MESH


def layer_kernel(
    sections, places, x_hbm, gain_hbm, w_hbm, bias_hbm, o_ref,
    main, rest, own, above, below, gain_ref, bias_ref, main_taps, rest_taps, normed, result, kept,
    load_sem, near_send, near_recv, first_send, far_send, far_recv, next_send, next_recv, done_send, done_recv,
):
    frames, rows, cols, chans = x_hbm.shape
    span = FRAMES
    turns = frames // span
    share = frames // sections
    pieces = share // span
    area = rows * cols
    size = span * area
    layer = lax.axis_index("section")
    place = lax.axis_index("row")
    last = sections - 1
    is_first = layer == 0
    is_last = layer == last
    core = lax.rem(place, 2)
    is_upper = core == 0
    is_lower = core == 1
    sibling = place + 1 - 2 * core
    beyond = place - 1 + 2 * core
    has_far = (beyond >= 0) & (beyond < places)
    no_far = jnp.logical_not(has_far)
    inner = rows - 1 - core * (rows - 1)
    outer = core * (rows - 1)

    low, high = pl.ds(0, LANES), pl.ds(LANES, chans - LANES)
    own_copies = [
        pltpu.make_async_copy(x_hbm.at[:, :, :, low], main, load_sem.at[0]),
        pltpu.make_async_copy(x_hbm.at[:, :, :, high], rest, load_sem.at[1]),
    ]
    weight_copies = [
        pltpu.make_async_copy(gain_hbm, gain_ref, load_sem.at[2]),
        pltpu.make_async_copy(bias_hbm, bias_ref, load_sem.at[3]),
        pltpu.make_async_copy(w_hbm.at[:, :, :, :, low], main_taps, load_sem.at[4]),
        pltpu.make_async_copy(w_hbm.at[:, :, :, :, high], rest_taps, load_sem.at[5]),
    ]

    @pl.when(is_first)
    def _():
        for copy in own_copies:
            copy.start()

    barrier = pltpu.get_barrier_semaphore()

    def greet(section, row):
        pl.semaphore_signal(barrier, inc=1, device_id=(section, row), device_id_type=MESH)

    source = jnp.maximum(layer - 1, 0)

    @pl.when(jnp.logical_not(is_first))
    def _():
        greet(source, place)

    @pl.when(has_far)
    def _():
        greet(source, beyond)

    greet(layer, sibling)

    @pl.when(jnp.logical_not(is_last))
    def _():
        greet(last, place)

    for copy in weight_copies:
        copy.start()

    def pack(first, second):
        middle = jnp.concatenate([first[..., LANES:], second[..., LANES:]], axis=-1)
        parts = [first[..., :LANES], middle, second[..., :LANES]]
        return jnp.concatenate([part.astype(jnp.bfloat16) for part in parts], axis=-2)

    def unpack(value):
        value = value.astype(jnp.float32)
        middle = value[..., cols : 2 * cols, :]
        rest = chans - LANES
        first = jnp.concatenate([value[..., 0:cols, :], middle[..., :rest]], axis=-1)
        second = jnp.concatenate([value[..., 2 * cols :, :], middle[..., rest:]], axis=-1)
        return jnp.stack([first, second])

    empty = jnp.zeros(above.shape, above.dtype)

    @pl.when(no_far & is_upper)
    def _():
        above[...] = empty

    @pl.when(no_far & is_lower)
    def _():
        below[...] = empty

    normed[0:span] = jnp.zeros((span,) + normed.shape[1:], normed.dtype)
    column = lax.rem(lax.broadcasted_iota(jnp.int32, (size, chans), 0), cols)

    @pl.when(is_first)
    def _():
        for copy in own_copies:
            copy.wait()
        large = main[...].reshape(turns, span, rows, cols, LANES)
        small = rest[...].astype(jnp.float32).reshape(turns, span, rows, cols, chans - LANES)
        middle = jnp.concatenate([small[:, 0], small[:, 1]], axis=-1).astype(jnp.bfloat16)
        own[...] = jnp.concatenate([large[:, 0], middle, large[:, 1]], axis=-2)

    far = has_far.astype(jnp.int32)
    first = is_first.astype(jnp.int32)
    final = is_last.astype(jnp.int32)
    pl.semaphore_wait(barrier, 1 + (1 - final) * (1 + far) + first * far + final * last)

    def send(src, dst, send_at, recv_at, section, row):
        return pltpu.make_async_remote_copy(
            src_ref=src, dst_ref=dst, send_sem=send_at, recv_sem=recv_at,
            device_id=(section, row), device_id_type=MESH,
        )

    def edge(turn, src, row, dst, sends, recvs, section, place_at):
        return send(src.at[turn, row], dst.at[turn], sends.at[turn], recvs.at[turn], section, place_at)

    def start_near(turn):
        @pl.when(is_upper)
        def _():
            edge(turn, own, rows - 1, above, near_send, near_recv, layer, sibling).start()

        @pl.when(is_lower)
        def _():
            edge(turn, own, 0, below, near_send, near_recv, layer, sibling).start()

    def start_far(turn, src, sends, section):
        @pl.when(has_far & is_upper)
        def _():
            edge(turn, src, 0, below, sends, far_recv, section, beyond).start()

        @pl.when(has_far & is_lower)
        def _():
            edge(turn, src, rows - 1, above, sends, far_recv, section, beyond).start()

    def near(turn):
        return edge(turn, own, 0, below, near_send, near_recv, layer, sibling)

    def distant(turn, sends=far_send):
        return edge(turn, own, 0, below, sends, far_recv, layer, beyond)

    def to_next(turn, row):
        return send(
            result.at[turn, row], own.at[turn, row], next_send.at[turn, row], next_recv.at[turn, row],
            layer + 1, place,
        )

    def to_keeper(turn):
        part = lax.rem(turn, pieces)
        return send(
            result.at[turn], kept.at[part], done_send.at[turn], done_recv.at[part], turn // pieces, place
        )

    @pl.when(is_first)
    def _():
        def begin(turn, carry):
            start_far(turn, own, first_send, layer)
            start_near(turn)
            return carry

        lax.fori_loop(0, turns, begin, 0)

    for copy in weight_copies:
        copy.wait()
    gain = gain_ref[...] * 0.5
    bias = bias_ref[...]

    def silu_norm(value):
        square = jnp.mean(value * value, axis=-1, keepdims=True)
        half = value * lax.rsqrt(square + 1e-06) * gain
        return half + half * jnp.tanh(half)

    def receive(turn):
        to_next(turn, inner).wait_recv()
        start_near(turn)
        to_next(turn, outer).wait_recv()

    @pl.when(jnp.logical_not(is_first))
    def _():
        receive(0)

    def advance(turn, carry):
        at = turn * span

        def mixed(out, places_of):
            for delay, dy in places_of:
                window = normed[delay : delay + span, dy : dy + rows].reshape(size, chans).astype(jnp.bfloat16)
                for dx in range(3):
                    tap = jnp.concatenate([main_taps[delay, dy, dx], rest_taps[delay, dy, dx]], axis=-1)
                    out[dx] = out[dx] + jnp.dot(window, tap, preferred_element_type=jnp.float32)
            return out

        state = unpack(own[turn]).reshape(size, chans)
        normed[span : 2 * span, 1 : rows + 1] = silu_norm(state).reshape(span, rows, cols, chans)
        zero = jnp.zeros((size, chans), jnp.float32)
        out = mixed([zero, state + bias, zero], [(0, 0), (0, 1), (0, 2), (1, 1), (2, 1)])

        @pl.when(jnp.logical_not(is_first) & (turn < turns - 1))
        def _():
            receive(turn + 1)

        @pl.when(has_far)
        def _():
            distant(turn).wait_recv()

        near(turn).wait_recv()

        border = unpack(jnp.stack([above[turn], below[turn]]))
        border = silu_norm(border.reshape(span * 2 * cols, chans)).reshape(span, 2, cols, chans)
        normed[span : 2 * span, 0] = border[:, 0]
        normed[span : 2 * span, rows + 1] = border[:, 1]
        out = mixed(out, [(1, 0), (2, 0), (1, 2), (2, 2)])
        normed[0:span] = normed[span : 2 * span]
        left = jnp.where(column == 0, 0.0, pltpu.roll(out[0], 1, 0))
        right = jnp.where(column == cols - 1, 0.0, pltpu.roll(out[2], size - 1, 0))
        output = (left + out[1] + right).reshape(span, rows, cols, chans)

        @pl.when(jnp.logical_not(is_last))
        def _():
            result[turn] = pack(output[0], output[1])
            to_next(turn, inner).start()
            to_next(turn, outer).start()
            start_far(turn, result, far_send, layer + 1)

        @pl.when(is_last & (turn // pieces < last))
        def _():
            result[turn] = pack(output[0], output[1])
            to_keeper(turn).start()

        @pl.when(is_last & (turn // pieces == last))
        def _():
            o_ref[pl.ds(at - last * share, span)] = output.astype(jnp.bfloat16)

        return carry

    lax.fori_loop(0, turns, advance, 0)

    @pl.when(is_last)
    def _():
        def drain(turn, carry):
            to_keeper(turn).wait_send()
            return carry

        lax.fori_loop(0, last * pieces, drain, 0)

    def drain(turn, carry):
        near(turn).wait_send()

        @pl.when(is_first & has_far)
        def _():
            distant(turn, first_send).wait_send()

        @pl.when(jnp.logical_not(is_last))
        def _():
            to_next(turn, 0).wait_send()
            to_next(turn, 1).wait_send()

            @pl.when(has_far)
            def _():
                distant(turn).wait_send()

        return carry

    lax.fori_loop(0, turns, drain, 0)

    @pl.when(jnp.logical_not(is_last))
    def _():
        def arrive(part, carry):
            to_keeper(part).wait_recv()
            o_ref[pl.ds(part * span, span)] = unpack(kept[part]).astype(jnp.bfloat16)
            return carry

        lax.fori_loop(0, pieces, arrive, 0)


def on_device(features, norm_gain, conv_weight, conv_bias):
    sections = lax.axis_size("section")
    places = lax.axis_size("row")
    frames, rows, cols, chans = features.shape
    share = frames // sections
    span = FRAMES
    turns = frames // span
    taps = conv_weight[0]
    anywhere = pl.BlockSpec(memory_space=pl.ANY)
    dma = pltpu.SemaphoreType.DMA
    half = jnp.bfloat16
    return pl.pallas_call(
        functools.partial(layer_kernel, sections, places),
        out_shape=pltpu.VMEM((share, rows, cols, chans), half),
        in_specs=[anywhere] * 4,
        out_specs=pl.BlockSpec(memory_space=pltpu.VMEM),
        scratch_shapes=[
            pltpu.VMEM((frames, rows, cols, LANES), half),
            pltpu.VMEM((frames, rows, cols, chans - LANES), half),
            pltpu.VMEM((turns, rows, 3 * cols, LANES), half),
            pltpu.VMEM((turns, 3 * cols, LANES), half),
            pltpu.VMEM((turns, 3 * cols, LANES), half),
            pltpu.VMEM(norm_gain.shape, jnp.float32),
            pltpu.VMEM(conv_bias.shape, jnp.float32),
            pltpu.VMEM((3, 3, 3, chans, LANES), half),
            pltpu.VMEM((3, 3, 3, chans, chans - LANES), half),
            pltpu.VMEM((2 * span, rows + 2, cols, chans), jnp.float32),
            pltpu.VMEM((turns, rows, 3 * cols, LANES), half),
            pltpu.VMEM((share // span, rows, 3 * cols, LANES), half),
            dma((6,)), dma((turns,)), dma((turns,)), dma((turns,)), dma((turns,)), dma((turns,)), dma((turns, rows)),
            dma((turns, rows)), dma((turns,)), dma((share // span,)),
        ],
        compiler_params=pltpu.CompilerParams(
            collective_id=0, has_side_effects=True, vmem_limit_bytes=60 * 1024 * 1024
        ),
    )(*(pltpu.with_memory_space_constraint(value, pltpu.HBM) for value in (features, norm_gain, taps, conv_bias)))


def solution(mesh):
    in_specs = (
        P(None, "row", None, None),
        P("section", None),
        P("section", None, None, None, None, None),
        P("section", None),
    )
    out_specs = P("section", "row", None, None)
    return jax.shard_map(
        on_device, mesh=mesh, in_specs=in_specs, out_specs=out_specs, check_vma=False
    )
```

```python
import functools

import jax
import jax.numpy as jnp
from jax import lax
from jax.experimental import pallas as pl
from jax.experimental.pallas import tpu as pltpu
from jax.sharding import PartitionSpec as P

FRAMES = 2
LANES = 128
MESH = pl.DeviceIdType.MESH


def layer_kernel(
    sections, places, x_hbm, gain_hbm, w_hbm, bias_hbm, o_ref,
    main, rest, own, above, below, gain_ref, bias_ref, main_taps, rest_taps, normed, result, kept,
    load_sem, near_send, near_recv, first_send, far_send, far_recv, next_send, next_recv, done_send, done_recv,
):
    frames, rows, cols, chans = x_hbm.shape
    span = FRAMES
    turns = frames // span
    share = frames // sections
    pieces = share // span
    area = rows * cols
    size = span * area
    layer = lax.axis_index("section")
    place = lax.axis_index("row")
    last = sections - 1
    is_first = layer == 0
    is_last = layer == last
    core = lax.rem(place, 2)
    is_upper = core == 0
    is_lower = core == 1
    sibling = place + 1 - 2 * core
    beyond = place - 1 + 2 * core
    has_far = (beyond >= 0) & (beyond < places)
    no_far = jnp.logical_not(has_far)
    inner = rows - 1 - core * (rows - 1)
    outer = core * (rows - 1)

    low, high = pl.ds(0, LANES), pl.ds(LANES, chans - LANES)
    own_copies = [
        pltpu.make_async_copy(x_hbm.at[:, :, :, low], main, load_sem.at[0]),
        pltpu.make_async_copy(x_hbm.at[:, :, :, high], rest, load_sem.at[1]),
    ]
    weight_copies = [
        pltpu.make_async_copy(gain_hbm, gain_ref, load_sem.at[2]),
        pltpu.make_async_copy(bias_hbm, bias_ref, load_sem.at[3]),
        pltpu.make_async_copy(w_hbm.at[:, :, :, :, low], main_taps, load_sem.at[4]),
        pltpu.make_async_copy(w_hbm.at[:, :, :, :, high], rest_taps, load_sem.at[5]),
    ]

    @pl.when(is_first)
    def _():
        for copy in own_copies:
            copy.start()

    barrier = pltpu.get_barrier_semaphore()

    def greet(section, row):
        pl.semaphore_signal(barrier, inc=1, device_id=(section, row), device_id_type=MESH)

    source = jnp.maximum(layer - 1, 0)

    @pl.when(jnp.logical_not(is_first))
    def _():
        greet(source, place)

    @pl.when(has_far)
    def _():
        greet(source, beyond)

    greet(layer, sibling)

    @pl.when(jnp.logical_not(is_last))
    def _():
        greet(last, place)

    for copy in weight_copies:
        copy.start()

    def pack(first, second):
        middle = jnp.concatenate([first[..., LANES:], second[..., LANES:]], axis=-1)
        parts = [first[..., :LANES], middle, second[..., :LANES]]
        return jnp.concatenate([part.astype(jnp.bfloat16) for part in parts], axis=-2)

    def unpack(value):
        value = value.astype(jnp.float32)
        middle = value[..., cols : 2 * cols, :]
        rest = chans - LANES
        first = jnp.concatenate([value[..., 0:cols, :], middle[..., :rest]], axis=-1)
        second = jnp.concatenate([value[..., 2 * cols :, :], middle[..., rest:]], axis=-1)
        return jnp.stack([first, second])

    empty = jnp.zeros(above.shape, above.dtype)

    @pl.when(no_far & is_upper)
    def _():
        above[...] = empty

    @pl.when(no_far & is_lower)
    def _():
        below[...] = empty

    normed[0:span] = jnp.zeros((span,) + normed.shape[1:], normed.dtype)
    column = lax.rem(lax.broadcasted_iota(jnp.int32, (size, chans), 0), cols)

    @pl.when(is_first)
    def _():
        for copy in own_copies:
            copy.wait()
        large = main[...].reshape(turns, span, rows, cols, LANES)
        small = rest[...].astype(jnp.float32).reshape(turns, span, rows, cols, chans - LANES)
        middle = jnp.concatenate([small[:, 0], small[:, 1]], axis=-1).astype(jnp.bfloat16)
        own[...] = jnp.concatenate([large[:, 0], middle, large[:, 1]], axis=-2)

    far = has_far.astype(jnp.int32)
    first = is_first.astype(jnp.int32)
    final = is_last.astype(jnp.int32)
    pl.semaphore_wait(barrier, 1 + (1 - final) * (1 + far) + first * far + final * last)

    def send(src, dst, send_at, recv_at, section, row):
        return pltpu.make_async_remote_copy(
            src_ref=src, dst_ref=dst, send_sem=send_at, recv_sem=recv_at,
            device_id=(section, row), device_id_type=MESH,
        )

    def edge(turn, src, row, dst, sends, recvs, section, place_at):
        return send(src.at[turn, row], dst.at[turn], sends.at[turn], recvs.at[turn], section, place_at)

    def start_near(turn):
        @pl.when(is_upper)
        def _():
            edge(turn, own, rows - 1, above, near_send, near_recv, layer, sibling).start()

        @pl.when(is_lower)
        def _():
            edge(turn, own, 0, below, near_send, near_recv, layer, sibling).start()

    def start_far(turn, src, sends, section):
        @pl.when(has_far & is_upper)
        def _():
            edge(turn, src, 0, below, sends, far_recv, section, beyond).start()

        @pl.when(has_far & is_lower)
        def _():
            edge(turn, src, rows - 1, above, sends, far_recv, section, beyond).start()

    def near(turn):
        return edge(turn, own, 0, below, near_send, near_recv, layer, sibling)

    def distant(turn, sends=far_send):
        return edge(turn, own, 0, below, sends, far_recv, layer, beyond)

    def to_next(turn, row):
        return send(
            result.at[turn, row], own.at[turn, row], next_send.at[turn, row], next_recv.at[turn, row],
            layer + 1, place,
        )

    def to_keeper(turn):
        part = lax.rem(turn, pieces)
        return send(
            result.at[turn], kept.at[part], done_send.at[turn], done_recv.at[part], turn // pieces, place
        )

    @pl.when(is_first)
    def _():
        def begin(turn, carry):
            start_far(turn, own, first_send, layer)
            start_near(turn)
            return carry

        lax.fori_loop(0, turns, begin, 0)

    for copy in weight_copies:
        copy.wait()
    gain = gain_ref[...] * 0.5
    bias = bias_ref[...]

    def silu_norm(value):
        square = jnp.mean(value * value, axis=-1, keepdims=True)
        half = value * lax.rsqrt(square + 1e-06) * gain
        return half + half * jnp.tanh(half)

    def receive(turn):
        to_next(turn, inner).wait_recv()
        start_near(turn)

    @pl.when(jnp.logical_not(is_first))
    def _():
        receive(0)

    def advance(turn, carry):
        at = turn * span

        def mixed(out, places_of):
            for delay, dy in places_of:
                window = normed[delay : delay + span, dy : dy + rows].reshape(size, chans).astype(jnp.bfloat16)
                for dx in range(3):
                    tap = jnp.concatenate([main_taps[delay, dy, dx], rest_taps[delay, dy, dx]], axis=-1)
                    out[dx] = out[dx] + jnp.dot(window, tap, preferred_element_type=jnp.float32)
            return out

        @pl.when(jnp.logical_not(is_first))
        def _():
            to_next(turn, outer).wait_recv()

        state = unpack(own[turn]).reshape(size, chans)
        normed[span : 2 * span, 1 : rows + 1] = silu_norm(state).reshape(span, rows, cols, chans)
        zero = jnp.zeros((size, chans), jnp.float32)
        out = mixed([zero, state + bias, zero], [(0, 0), (0, 1), (0, 2), (1, 1), (2, 1)])

        @pl.when(jnp.logical_not(is_first) & (turn < turns - 1))
        def _():
            receive(turn + 1)

        @pl.when(has_far)
        def _():
            distant(turn).wait_recv()

        near(turn).wait_recv()

        border = unpack(jnp.stack([above[turn], below[turn]]))
        border = silu_norm(border.reshape(span * 2 * cols, chans)).reshape(span, 2, cols, chans)
        normed[span : 2 * span, 0] = border[:, 0]
        normed[span : 2 * span, rows + 1] = border[:, 1]
        out = mixed(out, [(1, 0), (2, 0), (1, 2), (2, 2)])
        normed[0:span] = normed[span : 2 * span]
        left = jnp.where(column == 0, 0.0, pltpu.roll(out[0], 1, 0))
        right = jnp.where(column == cols - 1, 0.0, pltpu.roll(out[2], size - 1, 0))
        output = (left + out[1] + right).reshape(span, rows, cols, chans)

        @pl.when(jnp.logical_not(is_last))
        def _():
            result[turn] = pack(output[0], output[1])
            to_next(turn, inner).start()
            start_far(turn, result, far_send, layer + 1)
            to_next(turn, outer).start()

        @pl.when(is_last & (turn // pieces < last))
        def _():
            result[turn] = pack(output[0], output[1])
            to_keeper(turn).start()

        @pl.when(is_last & (turn // pieces == last))
        def _():
            o_ref[pl.ds(at - last * share, span)] = output.astype(jnp.bfloat16)

        return carry

    lax.fori_loop(0, turns, advance, 0)

    @pl.when(is_last)
    def _():
        def drain(turn, carry):
            to_keeper(turn).wait_send()
            return carry

        lax.fori_loop(0, last * pieces, drain, 0)

    def drain(turn, carry):
        near(turn).wait_send()

        @pl.when(is_first & has_far)
        def _():
            distant(turn, first_send).wait_send()

        @pl.when(jnp.logical_not(is_last))
        def _():
            to_next(turn, 0).wait_send()
            to_next(turn, 1).wait_send()

            @pl.when(has_far)
            def _():
                distant(turn).wait_send()

        return carry

    lax.fori_loop(0, turns, drain, 0)

    @pl.when(jnp.logical_not(is_last))
    def _():
        def arrive(part, carry):
            to_keeper(part).wait_recv()
            o_ref[pl.ds(part * span, span)] = unpack(kept[part]).astype(jnp.bfloat16)
            return carry

        lax.fori_loop(0, pieces, arrive, 0)


def on_device(features, norm_gain, conv_weight, conv_bias):
    sections = lax.axis_size("section")
    places = lax.axis_size("row")
    frames, rows, cols, chans = features.shape
    share = frames // sections
    span = FRAMES
    turns = frames // span
    taps = conv_weight[0]
    anywhere = pl.BlockSpec(memory_space=pl.ANY)
    dma = pltpu.SemaphoreType.DMA
    half = jnp.bfloat16
    return pl.pallas_call(
        functools.partial(layer_kernel, sections, places),
        out_shape=pltpu.VMEM((share, rows, cols, chans), half),
        in_specs=[anywhere] * 4,
        out_specs=pl.BlockSpec(memory_space=pltpu.VMEM),
        scratch_shapes=[
            pltpu.VMEM((frames, rows, cols, LANES), half),
            pltpu.VMEM((frames, rows, cols, chans - LANES), half),
            pltpu.VMEM((turns, rows, 3 * cols, LANES), half),
            pltpu.VMEM((turns, 3 * cols, LANES), half),
            pltpu.VMEM((turns, 3 * cols, LANES), half),
            pltpu.VMEM(norm_gain.shape, jnp.float32),
            pltpu.VMEM(conv_bias.shape, jnp.float32),
            pltpu.VMEM((3, 3, 3, chans, LANES), half),
            pltpu.VMEM((3, 3, 3, chans, chans - LANES), half),
            pltpu.VMEM((2 * span, rows + 2, cols, chans), jnp.float32),
            pltpu.VMEM((turns, rows, 3 * cols, LANES), half),
            pltpu.VMEM((share // span, rows, 3 * cols, LANES), half),
            dma((6,)), dma((turns,)), dma((turns,)), dma((turns,)), dma((turns,)), dma((turns,)), dma((turns, rows)),
            dma((turns, rows)), dma((turns,)), dma((share // span,)),
        ],
        compiler_params=pltpu.CompilerParams(
            collective_id=0, has_side_effects=True, vmem_limit_bytes=60 * 1024 * 1024
        ),
    )(*(pltpu.with_memory_space_constraint(value, pltpu.HBM) for value in (features, norm_gain, taps, conv_bias)))


def solution(mesh):
    in_specs = (
        P(None, "row", None, None),
        P("section", None),
        P("section", None, None, None, None, None),
        P("section", None),
    )
    out_specs = P("section", "row", None, None)
    return jax.shard_map(
        on_device, mesh=mesh, in_specs=in_specs, out_specs=out_specs, check_vma=False
    )
```

```python
import functools

import jax
import jax.numpy as jnp
from jax import lax
from jax.experimental import pallas as pl
from jax.experimental.pallas import tpu as pltpu
from jax.sharding import PartitionSpec as P

FRAMES = 2
LANES = 128
MESH = pl.DeviceIdType.MESH


def layer_kernel(
    sections, places, x_hbm, gain_hbm, w_hbm, bias_hbm, o_ref,
    main, rest, own, above, below, gain_ref, bias_ref, main_taps, rest_taps, normed, result, kept,
    load_sem, near_send, near_recv, first_send, far_send, far_recv, next_send, next_recv, done_send, done_recv,
):
    frames, rows, cols, chans = x_hbm.shape
    span = FRAMES
    turns = frames // span
    share = frames // sections
    pieces = share // span
    area = rows * cols
    size = span * area
    layer = lax.axis_index("section")
    place = lax.axis_index("row")
    last = sections - 1
    is_first = layer == 0
    is_last = layer == last
    core = lax.rem(place, 2)
    is_upper = core == 0
    is_lower = core == 1
    sibling = place + 1 - 2 * core
    beyond = place - 1 + 2 * core
    has_far = (beyond >= 0) & (beyond < places)
    no_far = jnp.logical_not(has_far)
    inner = rows - 1 - core * (rows - 1)
    outer = core * (rows - 1)

    low, high = pl.ds(0, LANES), pl.ds(LANES, chans - LANES)
    own_copies = [
        pltpu.make_async_copy(x_hbm.at[:, :, :, low], main, load_sem.at[0]),
        pltpu.make_async_copy(x_hbm.at[:, :, :, high], rest, load_sem.at[1]),
    ]
    weight_copies = [
        pltpu.make_async_copy(gain_hbm, gain_ref, load_sem.at[2]),
        pltpu.make_async_copy(bias_hbm, bias_ref, load_sem.at[3]),
        pltpu.make_async_copy(w_hbm.at[:, :, :, :, low], main_taps, load_sem.at[4]),
        pltpu.make_async_copy(w_hbm.at[:, :, :, :, high], rest_taps, load_sem.at[5]),
    ]

    @pl.when(is_first)
    def _():
        for copy in own_copies:
            copy.start()

    barrier = pltpu.get_barrier_semaphore()

    def greet(section, row):
        pl.semaphore_signal(barrier, inc=1, device_id=(section, row), device_id_type=MESH)

    source = jnp.maximum(layer - 1, 0)

    @pl.when(jnp.logical_not(is_first))
    def _():
        greet(source, place)

    @pl.when(has_far)
    def _():
        greet(source, beyond)

    greet(layer, sibling)

    @pl.when(jnp.logical_not(is_last))
    def _():
        greet(last, place)

    for copy in weight_copies:
        copy.start()

    def pack(first, second):
        middle = jnp.concatenate([first[..., LANES:], second[..., LANES:]], axis=-1)
        parts = [first[..., :LANES], middle, second[..., :LANES]]
        return jnp.concatenate([part.astype(jnp.bfloat16) for part in parts], axis=-2)

    def unpack(value):
        value = value.astype(jnp.float32)
        middle = value[..., cols : 2 * cols, :]
        rest = chans - LANES
        first = jnp.concatenate([value[..., 0:cols, :], middle[..., :rest]], axis=-1)
        second = jnp.concatenate([value[..., 2 * cols :, :], middle[..., rest:]], axis=-1)
        return jnp.stack([first, second])

    empty = jnp.zeros(above.shape, above.dtype)

    @pl.when(no_far & is_upper)
    def _():
        above[...] = empty

    @pl.when(no_far & is_lower)
    def _():
        below[...] = empty

    normed[0:span] = jnp.zeros((span,) + normed.shape[1:], normed.dtype)
    column = lax.rem(lax.broadcasted_iota(jnp.int32, (size, chans), 0), cols)

    @pl.when(is_first)
    def _():
        for copy in own_copies:
            copy.wait()
        large = main[...].reshape(turns, span, rows, cols, LANES)
        small = rest[...].astype(jnp.float32).reshape(turns, span, rows, cols, chans - LANES)
        middle = jnp.concatenate([small[:, 0], small[:, 1]], axis=-1).astype(jnp.bfloat16)
        own[...] = jnp.concatenate([large[:, 0], middle, large[:, 1]], axis=-2)

    far = has_far.astype(jnp.int32)
    first = is_first.astype(jnp.int32)
    final = is_last.astype(jnp.int32)
    pl.semaphore_wait(barrier, 1 + (1 - final) * (1 + far) + first * far + final * last)

    def send(src, dst, send_at, recv_at, section, row):
        return pltpu.make_async_remote_copy(
            src_ref=src, dst_ref=dst, send_sem=send_at, recv_sem=recv_at,
            device_id=(section, row), device_id_type=MESH,
        )

    def edge(turn, src, row, dst, sends, recvs, section, place_at):
        return send(src.at[turn, row], dst.at[turn], sends.at[turn], recvs.at[turn], section, place_at)

    def start_near(turn):
        @pl.when(is_upper)
        def _():
            edge(turn, own, rows - 1, above, near_send, near_recv, layer, sibling).start()

        @pl.when(is_lower)
        def _():
            edge(turn, own, 0, below, near_send, near_recv, layer, sibling).start()

    def start_far(turn, src, sends, section):
        @pl.when(has_far & is_upper)
        def _():
            edge(turn, src, 0, below, sends, far_recv, section, beyond).start()

        @pl.when(has_far & is_lower)
        def _():
            edge(turn, src, rows - 1, above, sends, far_recv, section, beyond).start()

    def near(turn):
        return edge(turn, own, 0, below, near_send, near_recv, layer, sibling)

    def distant(turn, sends=far_send):
        return edge(turn, own, 0, below, sends, far_recv, layer, beyond)

    def to_next(turn, row):
        return send(
            result.at[turn, row], own.at[turn, row], next_send.at[turn, row], next_recv.at[turn, row],
            layer + 1, place,
        )

    def to_keeper(turn):
        part = lax.rem(turn, pieces)
        return send(
            result.at[turn], kept.at[part], done_send.at[turn], done_recv.at[part], turn // pieces, place
        )

    @pl.when(is_first)
    def _():
        def begin(turn, carry):
            start_far(turn, own, first_send, layer)
            start_near(turn)
            return carry

        lax.fori_loop(0, turns, begin, 0)

    for copy in weight_copies:
        copy.wait()
    gain = gain_ref[...] * 0.5
    bias = bias_ref[...]

    def silu_norm(value):
        square = jnp.mean(value * value, axis=-1, keepdims=True)
        half = value * lax.rsqrt(square + 1e-06) * gain
        return half + half * jnp.tanh(half)

    def receive(turn):
        to_next(turn, inner).wait_recv()
        start_near(turn)

    @pl.when(jnp.logical_not(is_first))
    def _():
        receive(0)

    def advance(turn, carry):
        at = turn * span

        def mixed(out, places_of):
            for delay, dy in places_of:
                window = normed[delay : delay + span, dy : dy + rows].reshape(size, chans).astype(jnp.bfloat16)
                for dx in range(3):
                    tap = jnp.concatenate([main_taps[delay, dy, dx], rest_taps[delay, dy, dx]], axis=-1)
                    out[dx] = out[dx] + jnp.dot(window, tap, preferred_element_type=jnp.float32)
            return out

        @pl.when(jnp.logical_not(is_first))
        def _():
            to_next(turn, outer).wait_recv()

        state = unpack(own[turn]).reshape(size, chans)
        normed[span : 2 * span, 1 : rows + 1] = silu_norm(state).reshape(span, rows, cols, chans)
        zero = jnp.zeros((size, chans), jnp.float32)
        out = mixed([zero, state + bias, zero], [(0, 0), (0, 1), (0, 2), (1, 1), (2, 1)])

        @pl.when(jnp.logical_not(is_first) & (turn < turns - 1))
        def _():
            receive(turn + 1)

        @pl.when(has_far)
        def _():
            distant(turn).wait_recv()

        near(turn).wait_recv()

        border = unpack(jnp.stack([above[turn], below[turn]]))
        border = silu_norm(border.reshape(span * 2 * cols, chans)).reshape(span, 2, cols, chans)
        fresh = border.astype(jnp.bfloat16)
        for delay in (1, 2):
            for dy, row, kept_row in ((0, 0, 1), (2, 1, rows)):
                old = normed[delay : delay + span, kept_row].astype(jnp.bfloat16)
                if delay == 1:
                    edge_rows = jnp.stack([normed[1, dy // 2 * (rows + 1)].astype(jnp.bfloat16), fresh[0, row]])
                else:
                    edge_rows = fresh[:, row]
                pair = [edge_rows, old] if dy == 0 else [old, edge_rows]
                window = jnp.stack(pair, axis=1).reshape(size, chans)
                for dx in range(3):
                    tap = jnp.concatenate([main_taps[delay, dy, dx], rest_taps[delay, dy, dx]], axis=-1)
                    out[dx] = out[dx] + jnp.dot(window, tap, preferred_element_type=jnp.float32)
        left = jnp.where(column == 0, 0.0, pltpu.roll(out[0], 1, 0))
        right = jnp.where(column == cols - 1, 0.0, pltpu.roll(out[2], size - 1, 0))
        output = (left + out[1] + right).reshape(span, rows, cols, chans)

        @pl.when(jnp.logical_not(is_last))
        def _():
            result[turn] = pack(output[0], output[1])
            to_next(turn, inner).start()
            start_far(turn, result, far_send, layer + 1)
            to_next(turn, outer).start()

        @pl.when(is_last & (turn // pieces < last))
        def _():
            result[turn] = pack(output[0], output[1])
            to_keeper(turn).start()

        @pl.when(is_last & (turn // pieces == last))
        def _():
            o_ref[pl.ds(at - last * share, span)] = output.astype(jnp.bfloat16)

        normed[0:span, 1 : rows + 1] = normed[span : 2 * span, 1 : rows + 1]
        normed[0:span, 0] = border[:, 0]
        normed[0:span, rows + 1] = border[:, 1]
        return carry

    lax.fori_loop(0, turns, advance, 0)

    @pl.when(is_last)
    def _():
        def drain(turn, carry):
            to_keeper(turn).wait_send()
            return carry

        lax.fori_loop(0, last * pieces, drain, 0)

    def drain(turn, carry):
        near(turn).wait_send()

        @pl.when(is_first & has_far)
        def _():
            distant(turn, first_send).wait_send()

        @pl.when(jnp.logical_not(is_last))
        def _():
            to_next(turn, 0).wait_send()
            to_next(turn, 1).wait_send()

            @pl.when(has_far)
            def _():
                distant(turn).wait_send()

        return carry

    lax.fori_loop(0, turns, drain, 0)

    @pl.when(jnp.logical_not(is_last))
    def _():
        def arrive(part, carry):
            to_keeper(part).wait_recv()
            o_ref[pl.ds(part * span, span)] = unpack(kept[part]).astype(jnp.bfloat16)
            return carry

        lax.fori_loop(0, pieces, arrive, 0)


def on_device(features, norm_gain, conv_weight, conv_bias):
    sections = lax.axis_size("section")
    places = lax.axis_size("row")
    frames, rows, cols, chans = features.shape
    share = frames // sections
    span = FRAMES
    turns = frames // span
    taps = conv_weight[0]
    anywhere = pl.BlockSpec(memory_space=pl.ANY)
    dma = pltpu.SemaphoreType.DMA
    half = jnp.bfloat16
    return pl.pallas_call(
        functools.partial(layer_kernel, sections, places),
        out_shape=pltpu.VMEM((share, rows, cols, chans), half),
        in_specs=[anywhere] * 4,
        out_specs=pl.BlockSpec(memory_space=pltpu.VMEM),
        scratch_shapes=[
            pltpu.VMEM((frames, rows, cols, LANES), half),
            pltpu.VMEM((frames, rows, cols, chans - LANES), half),
            pltpu.VMEM((turns, rows, 3 * cols, LANES), half),
            pltpu.VMEM((turns, 3 * cols, LANES), half),
            pltpu.VMEM((turns, 3 * cols, LANES), half),
            pltpu.VMEM(norm_gain.shape, jnp.float32),
            pltpu.VMEM(conv_bias.shape, jnp.float32),
            pltpu.VMEM((3, 3, 3, chans, LANES), half),
            pltpu.VMEM((3, 3, 3, chans, chans - LANES), half),
            pltpu.VMEM((2 * span, rows + 2, cols, chans), jnp.float32),
            pltpu.VMEM((turns, rows, 3 * cols, LANES), half),
            pltpu.VMEM((share // span, rows, 3 * cols, LANES), half),
            dma((6,)), dma((turns,)), dma((turns,)), dma((turns,)), dma((turns,)), dma((turns,)), dma((turns, rows)),
            dma((turns, rows)), dma((turns,)), dma((share // span,)),
        ],
        compiler_params=pltpu.CompilerParams(
            collective_id=0, has_side_effects=True, vmem_limit_bytes=60 * 1024 * 1024
        ),
    )(*(pltpu.with_memory_space_constraint(value, pltpu.HBM) for value in (features, norm_gain, taps, conv_bias)))


def solution(mesh):
    in_specs = (
        P(None, "row", None, None),
        P("section", None),
        P("section", None, None, None, None, None),
        P("section", None),
    )
    out_specs = P("section", "row", None, None)
    return jax.shard_map(
        on_device, mesh=mesh, in_specs=in_specs, out_specs=out_specs, check_vma=False
    )
```

```python
import functools

import jax
import jax.numpy as jnp
from jax import lax
from jax.experimental import pallas as pl
from jax.experimental.pallas import tpu as pltpu
from jax.sharding import PartitionSpec as P

FRAMES = 2
LANES = 128
MESH = pl.DeviceIdType.MESH


def layer_kernel(
    sections, places, x_hbm, gain_hbm, w_hbm, bias_hbm, o_ref,
    main, rest, own, above, below, gain_ref, bias_ref, main_taps, rest_taps, normed, result, kept,
    load_sem, near_send, near_recv, first_send, far_send, far_recv, next_send, next_recv, done_send, done_recv,
):
    frames, rows, cols, chans = x_hbm.shape
    span = FRAMES
    turns = frames // span
    share = frames // sections
    pieces = share // span
    area = rows * cols
    size = span * area
    layer = lax.axis_index("section")
    place = lax.axis_index("row")
    last = sections - 1
    is_first = layer == 0
    is_last = layer == last
    core = lax.rem(place, 2)
    is_upper = core == 0
    is_lower = core == 1
    sibling = place + 1 - 2 * core
    beyond = place - 1 + 2 * core
    has_far = (beyond >= 0) & (beyond < places)
    no_far = jnp.logical_not(has_far)
    inner = rows - 1 - core * (rows - 1)
    outer = core * (rows - 1)

    low, high = pl.ds(0, LANES), pl.ds(LANES, chans - LANES)
    own_copies = [
        pltpu.make_async_copy(x_hbm.at[:, :, :, low], main, load_sem.at[0]),
        pltpu.make_async_copy(x_hbm.at[:, :, :, high], rest, load_sem.at[1]),
    ]
    weight_copies = [
        pltpu.make_async_copy(gain_hbm, gain_ref, load_sem.at[2]),
        pltpu.make_async_copy(bias_hbm, bias_ref, load_sem.at[3]),
        pltpu.make_async_copy(w_hbm.at[:, :, :, :, low], main_taps, load_sem.at[4]),
        pltpu.make_async_copy(w_hbm.at[:, :, :, :, high], rest_taps, load_sem.at[5]),
    ]

    barrier = pltpu.get_barrier_semaphore()

    def greet(section, row):
        pl.semaphore_signal(barrier, inc=1, device_id=(section, row), device_id_type=MESH)

    source = jnp.maximum(layer - 1, 0)

    @pl.when(jnp.logical_not(is_first))
    def _():
        greet(source, place)

    @pl.when(has_far)
    def _():
        greet(source, beyond)

    greet(layer, sibling)

    @pl.when(jnp.logical_not(is_last))
    def _():
        greet(last, place)

    @pl.when(is_first)
    def _():
        for copy in own_copies:
            copy.start()

    for copy in weight_copies:
        copy.start()

    def pack(first, second):
        middle = jnp.concatenate([first[..., LANES:], second[..., LANES:]], axis=-1)
        parts = [first[..., :LANES], middle, second[..., :LANES]]
        return jnp.concatenate([part.astype(jnp.bfloat16) for part in parts], axis=-2)

    def unpack(value):
        value = value.astype(jnp.float32)
        middle = value[..., cols : 2 * cols, :]
        rest = chans - LANES
        first = jnp.concatenate([value[..., 0:cols, :], middle[..., :rest]], axis=-1)
        second = jnp.concatenate([value[..., 2 * cols :, :], middle[..., rest:]], axis=-1)
        return jnp.stack([first, second])

    empty = jnp.zeros(above.shape, above.dtype)

    @pl.when(no_far & is_upper)
    def _():
        above[...] = empty

    @pl.when(no_far & is_lower)
    def _():
        below[...] = empty

    normed[0:span] = jnp.zeros((span,) + normed.shape[1:], normed.dtype)
    column = lax.rem(lax.broadcasted_iota(jnp.int32, (size, chans), 0), cols)

    def arrange(start, count):
        large = main[start * span : (start + count) * span].reshape(count, span, rows, cols, LANES)
        small = rest[start * span : (start + count) * span].astype(jnp.float32)
        small = small.reshape(count, span, rows, cols, chans - LANES)
        middle = jnp.concatenate([small[:, 0], small[:, 1]], axis=-1).astype(jnp.bfloat16)
        own[start : start + count] = jnp.concatenate([large[:, 0], middle, large[:, 1]], axis=-2)

    @pl.when(is_first)
    def _():
        for copy in own_copies:
            copy.wait()
        arrange(0, 1)

    far = has_far.astype(jnp.int32)
    first = is_first.astype(jnp.int32)
    final = is_last.astype(jnp.int32)
    pl.semaphore_wait(barrier, 1 + (1 - final) * (1 + far) + first * far + final * last)

    def send(src, dst, send_at, recv_at, section, row):
        return pltpu.make_async_remote_copy(
            src_ref=src, dst_ref=dst, send_sem=send_at, recv_sem=recv_at,
            device_id=(section, row), device_id_type=MESH,
        )

    def edge(turn, src, row, dst, sends, recvs, section, place_at):
        return send(src.at[turn, row], dst.at[turn], sends.at[turn], recvs.at[turn], section, place_at)

    def start_near(turn):
        @pl.when(is_upper)
        def _():
            edge(turn, own, rows - 1, above, near_send, near_recv, layer, sibling).start()

        @pl.when(is_lower)
        def _():
            edge(turn, own, 0, below, near_send, near_recv, layer, sibling).start()

    def start_far(turn, src, sends, section):
        @pl.when(has_far & is_upper)
        def _():
            edge(turn, src, 0, below, sends, far_recv, section, beyond).start()

        @pl.when(has_far & is_lower)
        def _():
            edge(turn, src, rows - 1, above, sends, far_recv, section, beyond).start()

    def near(turn):
        return edge(turn, own, 0, below, near_send, near_recv, layer, sibling)

    def distant(turn, sends=far_send):
        return edge(turn, own, 0, below, sends, far_recv, layer, beyond)

    def to_next(turn, row):
        return send(
            result.at[turn, row], own.at[turn, row], next_send.at[turn, row], next_recv.at[turn, row],
            layer + 1, place,
        )

    def to_keeper(turn):
        part = lax.rem(turn, pieces)
        return send(
            result.at[turn], kept.at[part], done_send.at[turn], done_recv.at[part], turn // pieces, place
        )

    @pl.when(is_first)
    def _():
        def begin(turn, carry):
            start_far(turn, own, first_send, layer)
            start_near(turn)
            return carry

        begin(0, 0)
        arrange(1, turns - 1)
        lax.fori_loop(1, turns, begin, 0)

    for copy in weight_copies:
        copy.wait()
    gain = gain_ref[...] * 0.5
    bias = bias_ref[...]

    def silu_norm(value):
        square = jnp.mean(value * value, axis=-1, keepdims=True)
        half = value * lax.rsqrt(square + 1e-06) * gain
        return half + half * jnp.tanh(half)

    def receive(turn):
        to_next(turn, inner).wait_recv()
        start_near(turn)

    @pl.when(jnp.logical_not(is_first))
    def _():
        receive(0)

    def advance(turn, carry):
        at = turn * span

        def mixed(out, places_of):
            for delay, dy in places_of:
                window = normed[delay : delay + span, dy : dy + rows].reshape(size, chans).astype(jnp.bfloat16)
                for dx in range(3):
                    tap = jnp.concatenate([main_taps[delay, dy, dx], rest_taps[delay, dy, dx]], axis=-1)
                    out[dx] = out[dx] + jnp.dot(window, tap, preferred_element_type=jnp.float32)
            return out

        @pl.when(jnp.logical_not(is_first))
        def _():
            to_next(turn, outer).wait_recv()

        state = unpack(own[turn]).reshape(size, chans)
        middle = silu_norm(state).reshape(span, rows, cols, chans)
        normed[span : 2 * span, 1 : rows + 1] = middle
        middle = middle.astype(jnp.bfloat16)
        zero = jnp.zeros((size, chans), jnp.float32)
        out = mixed([zero, state + bias, zero], [(0, 0), (0, 1), (0, 2)])
        earlier = jnp.stack([normed[1, 1 : rows + 1].astype(jnp.bfloat16), middle[0]])
        for delay, window in ((1, earlier), (2, middle)):
            for dx in range(3):
                tap = jnp.concatenate([main_taps[delay, 1, dx], rest_taps[delay, 1, dx]], axis=-1)
                out[dx] = out[dx] + jnp.dot(window.reshape(size, chans), tap, preferred_element_type=jnp.float32)

        @pl.when(jnp.logical_not(is_first) & (turn < turns - 1))
        def _():
            receive(turn + 1)

        @pl.when(has_far)
        def _():
            distant(turn).wait_recv()

        near(turn).wait_recv()

        border = unpack(jnp.stack([above[turn], below[turn]]))
        border = silu_norm(border.reshape(span * 2 * cols, chans)).reshape(span, 2, cols, chans)
        fresh = border.astype(jnp.bfloat16)
        for delay in (1, 2):
            for dy, row, kept_row in ((0, 0, 1), (2, 1, rows)):
                old = normed[delay : delay + span, kept_row].astype(jnp.bfloat16)
                if delay == 1:
                    edge_rows = jnp.stack([normed[1, dy // 2 * (rows + 1)].astype(jnp.bfloat16), fresh[0, row]])
                else:
                    edge_rows = fresh[:, row]
                pair = [edge_rows, old] if dy == 0 else [old, edge_rows]
                window = jnp.stack(pair, axis=1).reshape(size, chans)
                for dx in range(3):
                    tap = jnp.concatenate([main_taps[delay, dy, dx], rest_taps[delay, dy, dx]], axis=-1)
                    out[dx] = out[dx] + jnp.dot(window, tap, preferred_element_type=jnp.float32)
        left = jnp.where(column == 0, 0.0, pltpu.roll(out[0], 1, 0))
        right = jnp.where(column == cols - 1, 0.0, pltpu.roll(out[2], size - 1, 0))
        output = (left + out[1] + right).reshape(span, rows, cols, chans)

        @pl.when(jnp.logical_not(is_last))
        def _():
            result[turn] = pack(output[0], output[1])
            to_next(turn, inner).start()
            start_far(turn, result, far_send, layer + 1)
            to_next(turn, outer).start()

        @pl.when(is_last & (turn // pieces < last))
        def _():
            result[turn] = pack(output[0], output[1])
            to_keeper(turn).start()

        @pl.when(is_last & (turn // pieces == last))
        def _():
            o_ref[pl.ds(at - last * share, span)] = output.astype(jnp.bfloat16)

        normed[0:span, 1 : rows + 1] = normed[span : 2 * span, 1 : rows + 1]
        normed[0:span, 0] = border[:, 0]
        normed[0:span, rows + 1] = border[:, 1]
        return carry

    lax.fori_loop(0, turns, advance, 0)

    @pl.when(is_last)
    def _():
        def drain(turn, carry):
            to_keeper(turn).wait_send()
            return carry

        lax.fori_loop(0, last * pieces, drain, 0)

    def drain(turn, carry):
        near(turn).wait_send()

        @pl.when(is_first & has_far)
        def _():
            distant(turn, first_send).wait_send()

        @pl.when(jnp.logical_not(is_last))
        def _():
            to_next(turn, 0).wait_send()
            to_next(turn, 1).wait_send()

            @pl.when(has_far)
            def _():
                distant(turn).wait_send()

        return carry

    lax.fori_loop(0, turns, drain, 0)

    @pl.when(jnp.logical_not(is_last))
    def _():
        def arrive(part, carry):
            to_keeper(part).wait_recv()
            o_ref[pl.ds(part * span, span)] = unpack(kept[part]).astype(jnp.bfloat16)
            return carry

        lax.fori_loop(0, pieces, arrive, 0)


def on_device(features, norm_gain, conv_weight, conv_bias):
    sections = lax.axis_size("section")
    places = lax.axis_size("row")
    frames, rows, cols, chans = features.shape
    share = frames // sections
    span = FRAMES
    turns = frames // span
    taps = conv_weight[0]
    anywhere = pl.BlockSpec(memory_space=pl.ANY)
    dma = pltpu.SemaphoreType.DMA
    half = jnp.bfloat16
    return pl.pallas_call(
        functools.partial(layer_kernel, sections, places),
        out_shape=pltpu.VMEM((share, rows, cols, chans), half),
        in_specs=[anywhere] * 4,
        out_specs=pl.BlockSpec(memory_space=pltpu.VMEM),
        scratch_shapes=[
            pltpu.VMEM((frames, rows, cols, LANES), half),
            pltpu.VMEM((frames, rows, cols, chans - LANES), half),
            pltpu.VMEM((turns, rows, 3 * cols, LANES), half),
            pltpu.VMEM((turns, 3 * cols, LANES), half),
            pltpu.VMEM((turns, 3 * cols, LANES), half),
            pltpu.VMEM(norm_gain.shape, jnp.float32),
            pltpu.VMEM(conv_bias.shape, jnp.float32),
            pltpu.VMEM((3, 3, 3, chans, LANES), half),
            pltpu.VMEM((3, 3, 3, chans, chans - LANES), half),
            pltpu.VMEM((2 * span, rows + 2, cols, chans), jnp.float32),
            pltpu.VMEM((turns, rows, 3 * cols, LANES), half),
            pltpu.VMEM((share // span, rows, 3 * cols, LANES), half),
            dma((6,)), dma((turns,)), dma((turns,)), dma((turns,)), dma((turns,)), dma((turns,)), dma((turns, rows)),
            dma((turns, rows)), dma((turns,)), dma((share // span,)),
        ],
        compiler_params=pltpu.CompilerParams(
            collective_id=0, has_side_effects=True, vmem_limit_bytes=60 * 1024 * 1024
        ),
    )(*(pltpu.with_memory_space_constraint(value, pltpu.HBM) for value in (features, norm_gain, taps, conv_bias)))


def solution(mesh):
    in_specs = (
        P(None, "row", None, None),
        P("section", None),
        P("section", None, None, None, None, None),
        P("section", None),
    )
    out_specs = P("section", "row", None, None)
    return jax.shard_map(
        on_device, mesh=mesh, in_specs=in_specs, out_specs=out_specs, check_vma=False
    )
```

```python
import functools

import jax
import jax.numpy as jnp
from jax import lax
from jax.experimental import pallas as pl
from jax.experimental.pallas import tpu as pltpu
from jax.sharding import PartitionSpec as P

FRAMES = 2
LANES = 128
MESH = pl.DeviceIdType.MESH


def layer_kernel(
    sections, places, x_hbm, gain_hbm, w_hbm, bias_hbm, o_ref,
    main, rest, own, above, below, gain_ref, bias_ref, main_taps, rest_taps, normed, result, kept,
    load_sem, near_send, near_recv, first_send, far_send, far_recv, next_send, next_recv, done_send, done_recv,
):
    frames, rows, cols, chans = x_hbm.shape
    span = FRAMES
    turns = frames // span
    share = frames // sections
    pieces = share // span
    area = rows * cols
    size = span * area
    layer = lax.axis_index("section")
    place = lax.axis_index("row")
    last = sections - 1
    is_first = layer == 0
    is_last = layer == last
    core = lax.rem(place, 2)
    is_upper = core == 0
    is_lower = core == 1
    sibling = place + 1 - 2 * core
    beyond = place - 1 + 2 * core
    has_far = (beyond >= 0) & (beyond < places)
    no_far = jnp.logical_not(has_far)
    inner = rows - 1 - core * (rows - 1)
    outer = core * (rows - 1)

    low, high = pl.ds(0, LANES), pl.ds(LANES, chans - LANES)
    own_copies = [
        pltpu.make_async_copy(x_hbm.at[:, :, :, low], main, load_sem.at[0]),
        pltpu.make_async_copy(x_hbm.at[:, :, :, high], rest, load_sem.at[1]),
    ]
    weight_copies = [
        pltpu.make_async_copy(gain_hbm, gain_ref, load_sem.at[2]),
        pltpu.make_async_copy(bias_hbm, bias_ref, load_sem.at[3]),
        pltpu.make_async_copy(w_hbm.at[:, :, :, :, low], main_taps, load_sem.at[4]),
        pltpu.make_async_copy(w_hbm.at[:, :, :, :, high], rest_taps, load_sem.at[5]),
    ]

    @pl.when(is_first)
    def _():
        for copy in own_copies:
            copy.start()

    barrier = pltpu.get_barrier_semaphore()

    def greet(section, row):
        pl.semaphore_signal(barrier, inc=1, device_id=(section, row), device_id_type=MESH)

    source = jnp.maximum(layer - 1, 0)

    @pl.when(jnp.logical_not(is_first))
    def _():
        greet(source, place)

    @pl.when(has_far)
    def _():
        greet(source, beyond)

    greet(layer, sibling)

    @pl.when(jnp.logical_not(is_last))
    def _():
        greet(last, place)

    for copy in weight_copies:
        copy.start()

    def pack(first, second):
        middle = jnp.concatenate([first[..., LANES:], second[..., LANES:]], axis=-1)
        parts = [first[..., :LANES], middle, second[..., :LANES]]
        return jnp.concatenate([part.astype(jnp.bfloat16) for part in parts], axis=-2)

    def unpack(value):
        value = value.astype(jnp.float32)
        middle = value[..., cols : 2 * cols, :]
        rest = chans - LANES
        first = jnp.concatenate([value[..., 0:cols, :], middle[..., :rest]], axis=-1)
        second = jnp.concatenate([value[..., 2 * cols :, :], middle[..., rest:]], axis=-1)
        return jnp.stack([first, second])

    empty = jnp.zeros(above.shape, above.dtype)

    @pl.when(no_far & is_upper)
    def _():
        above[...] = empty

    @pl.when(no_far & is_lower)
    def _():
        below[...] = empty

    normed[0:span] = jnp.zeros((span,) + normed.shape[1:], normed.dtype)
    column = lax.rem(lax.broadcasted_iota(jnp.int32, (size, chans), 0), cols)

    @pl.when(is_first)
    def _():
        for copy in own_copies:
            copy.wait()
        large = main[...].reshape(turns, span, rows, cols, LANES)
        small = rest[...].astype(jnp.float32).reshape(turns, span, rows, cols, chans - LANES)
        middle = jnp.concatenate([small[:, 0], small[:, 1]], axis=-1).astype(jnp.bfloat16)
        own[...] = jnp.concatenate([large[:, 0], middle, large[:, 1]], axis=-2)

    far = has_far.astype(jnp.int32)
    first = is_first.astype(jnp.int32)
    final = is_last.astype(jnp.int32)
    pl.semaphore_wait(barrier, 1 + (1 - final) * (1 + far) + first * far + final * last)

    def send(src, dst, send_at, recv_at, section, row):
        return pltpu.make_async_remote_copy(
            src_ref=src, dst_ref=dst, send_sem=send_at, recv_sem=recv_at,
            device_id=(section, row), device_id_type=MESH,
        )

    def edge(turn, src, row, dst, sends, recvs, section, place_at):
        return send(src.at[turn, row], dst.at[turn], sends.at[turn], recvs.at[turn], section, place_at)

    def start_near(turn):
        @pl.when(is_upper)
        def _():
            edge(turn, own, rows - 1, above, near_send, near_recv, layer, sibling).start()

        @pl.when(is_lower)
        def _():
            edge(turn, own, 0, below, near_send, near_recv, layer, sibling).start()

    def start_far(turn, src, sends, section):
        @pl.when(has_far & is_upper)
        def _():
            edge(turn, src, 0, below, sends, far_recv, section, beyond).start()

        @pl.when(has_far & is_lower)
        def _():
            edge(turn, src, rows - 1, above, sends, far_recv, section, beyond).start()

    def near(turn):
        return edge(turn, own, 0, below, near_send, near_recv, layer, sibling)

    def distant(turn, sends=far_send):
        return edge(turn, own, 0, below, sends, far_recv, layer, beyond)

    def to_next(turn, row):
        return send(
            result.at[turn, row], own.at[turn, row], next_send.at[turn, row], next_recv.at[turn, row],
            layer + 1, place,
        )

    def to_keeper(turn):
        part = lax.rem(turn, pieces)
        return send(
            result.at[turn], kept.at[part], done_send.at[turn], done_recv.at[part], turn // pieces, place
        )

    @pl.when(is_first)
    def _():
        def begin(turn, carry):
            start_far(turn, own, first_send, layer)
            start_near(turn)
            return carry

        lax.fori_loop(0, turns, begin, 0)

    for copy in weight_copies:
        copy.wait()
    gain = gain_ref[...] * 0.5
    bias = bias_ref[...]

    def silu_norm(value):
        square = jnp.mean(value * value, axis=-1, keepdims=True)
        half = value * lax.rsqrt(square + 1e-06) * gain
        return half + half * jnp.tanh(half)

    def receive(turn):
        to_next(turn, inner).wait_recv()
        start_near(turn)

    @pl.when(jnp.logical_not(is_first))
    def _():
        receive(0)

    def advance(turn, carry):
        at = turn * span

        def mixed(out, places_of):
            for delay, dy in places_of:
                window = normed[delay : delay + span, dy : dy + rows].reshape(size, chans).astype(jnp.bfloat16)
                for dx in range(3):
                    tap = jnp.concatenate([main_taps[delay, dy, dx], rest_taps[delay, dy, dx]], axis=-1)
                    out[dx] = out[dx] + jnp.dot(window, tap, preferred_element_type=jnp.float32)
            return out

        @pl.when(jnp.logical_not(is_first))
        def _():
            to_next(turn, outer).wait_recv()

        state = unpack(own[turn]).reshape(size, chans)
        normed[span : 2 * span, 1 : rows + 1] = silu_norm(state).reshape(span, rows, cols, chans)
        zero = jnp.zeros((size, chans), jnp.float32)
        out = mixed([zero, state + bias, zero], [(0, 0), (0, 1), (0, 2), (1, 1), (2, 1)])

        @pl.when(jnp.logical_not(is_first) & (turn < turns - 1))
        def _():
            receive(turn + 1)

        @pl.when(has_far)
        def _():
            distant(turn).wait_recv()

        near(turn).wait_recv()

        border = unpack(jnp.stack([above[turn], below[turn]]))
        border = silu_norm(border.reshape(span * 2 * cols, chans)).reshape(span, 2, cols, chans)
        fresh = border.astype(jnp.bfloat16)
        for delay in (1, 2):
            for dy, row, kept_row in ((0, 0, 1), (2, 1, rows)):
                old = normed[delay : delay + span, kept_row].astype(jnp.bfloat16)
                if delay == 1:
                    edge_rows = jnp.stack([normed[1, dy // 2 * (rows + 1)].astype(jnp.bfloat16), fresh[0, row]])
                else:
                    edge_rows = fresh[:, row]
                pair = [edge_rows, old] if dy == 0 else [old, edge_rows]
                window = jnp.stack(pair, axis=1).reshape(size, chans)
                for dx in range(3):
                    tap = jnp.concatenate([main_taps[delay, dy, dx], rest_taps[delay, dy, dx]], axis=-1)
                    out[dx] = out[dx] + jnp.dot(window, tap, preferred_element_type=jnp.float32)
        left = jnp.where(column == 0, 0.0, pltpu.roll(out[0], 1, 0))
        right = jnp.where(column == cols - 1, 0.0, pltpu.roll(out[2], size - 1, 0))
        output = (left + out[1] + right).reshape(span, rows, cols, chans)

        result[turn] = pack(output[0], output[1])

        @pl.when(jnp.logical_not(is_last))
        def _():
            to_next(turn, inner).start()
            start_far(turn, result, far_send, layer + 1)
            to_next(turn, outer).start()

        @pl.when(is_last & (turn // pieces < last))
        def _():
            to_keeper(turn).start()

        @pl.when(is_last & (turn // pieces == last))
        def _():
            o_ref[pl.ds(at - last * share, span)] = output.astype(jnp.bfloat16)

        normed[0:span, 1 : rows + 1] = normed[span : 2 * span, 1 : rows + 1]
        normed[0:span, 0] = border[:, 0]
        normed[0:span, rows + 1] = border[:, 1]
        return carry

    lax.fori_loop(0, turns, advance, 0)

    @pl.when(is_last)
    def _():
        def drain(turn, carry):
            to_keeper(turn).wait_send()
            return carry

        lax.fori_loop(0, last * pieces, drain, 0)

    def drain(turn, carry):
        near(turn).wait_send()

        @pl.when(is_first & has_far)
        def _():
            distant(turn, first_send).wait_send()

        @pl.when(jnp.logical_not(is_last))
        def _():
            to_next(turn, 0).wait_send()
            to_next(turn, 1).wait_send()

            @pl.when(has_far)
            def _():
                distant(turn).wait_send()

        return carry

    lax.fori_loop(0, turns, drain, 0)

    @pl.when(jnp.logical_not(is_last))
    def _():
        def arrive(part, carry):
            to_keeper(part).wait_recv()
            o_ref[pl.ds(part * span, span)] = unpack(kept[part]).astype(jnp.bfloat16)
            return carry

        lax.fori_loop(0, pieces, arrive, 0)


def on_device(features, norm_gain, conv_weight, conv_bias):
    sections = lax.axis_size("section")
    places = lax.axis_size("row")
    frames, rows, cols, chans = features.shape
    share = frames // sections
    span = FRAMES
    turns = frames // span
    taps = conv_weight[0]
    anywhere = pl.BlockSpec(memory_space=pl.ANY)
    dma = pltpu.SemaphoreType.DMA
    half = jnp.bfloat16
    return pl.pallas_call(
        functools.partial(layer_kernel, sections, places),
        out_shape=pltpu.VMEM((share, rows, cols, chans), half),
        in_specs=[anywhere] * 4,
        out_specs=pl.BlockSpec(memory_space=pltpu.VMEM),
        scratch_shapes=[
            pltpu.VMEM((frames, rows, cols, LANES), half),
            pltpu.VMEM((frames, rows, cols, chans - LANES), half),
            pltpu.VMEM((turns, rows, 3 * cols, LANES), half),
            pltpu.VMEM((turns, 3 * cols, LANES), half),
            pltpu.VMEM((turns, 3 * cols, LANES), half),
            pltpu.VMEM(norm_gain.shape, jnp.float32),
            pltpu.VMEM(conv_bias.shape, jnp.float32),
            pltpu.VMEM((3, 3, 3, chans, LANES), half),
            pltpu.VMEM((3, 3, 3, chans, chans - LANES), half),
            pltpu.VMEM((2 * span, rows + 2, cols, chans), jnp.float32),
            pltpu.VMEM((turns, rows, 3 * cols, LANES), half),
            pltpu.VMEM((share // span, rows, 3 * cols, LANES), half),
            dma((6,)), dma((turns,)), dma((turns,)), dma((turns,)), dma((turns,)), dma((turns,)), dma((turns, rows)),
            dma((turns, rows)), dma((turns,)), dma((share // span,)),
        ],
        compiler_params=pltpu.CompilerParams(
            collective_id=0, has_side_effects=True, vmem_limit_bytes=60 * 1024 * 1024
        ),
    )(*(pltpu.with_memory_space_constraint(value, pltpu.HBM) for value in (features, norm_gain, taps, conv_bias)))


def solution(mesh):
    in_specs = (
        P(None, "row", None, None),
        P("section", None),
        P("section", None, None, None, None, None),
        P("section", None),
    )
    out_specs = P("section", "row", None, None)
    return jax.shard_map(
        on_device, mesh=mesh, in_specs=in_specs, out_specs=out_specs, check_vma=False
    )
```
